32 devices in a mesh: poles: 2 (over x), row: 8 (over z, y), col: 2 (over core).
Axes of the slice: x: 2, y: 2, z: 4, core: 2. Of those that a mesh axis runs over, the one named last changes fastest.
Arguments:
- root_inverse: bfloat16 [16384, 8192], P(('poles', 'row'), 'col'), parts along dimension 0, may hold values from -6 to 6
- panels: bfloat16 [4, 1024, 8192], P(('poles', 'col'), None, 'row'), parts along dimension 0, may hold values from -0.1875 to 0.1875
- diag_inverse: bfloat16 [4, 8192, 8192], P(('poles', 'col'), 'row'), parts along dimension 0, may hold values from -6 to 6
- row_lists: int32 [2, 1024], replicated, may hold values from 0 to 8191, as said below
Outputs:
- offdiag_inverse: bfloat16 [4, 1024, 8192], P(('poles', 'col'), None, 'row'), parts along dimension 0
- diag_result: bfloat16 [4, 8192, 8192], P(('poles', 'col'), 'row'), parts along dimension 0
The draws below stay inside these ranges and needn't reach their ends.
There are 2 independent parts, one for each index of `poles`. The reference program is written for one: setup_inputs(seed, part) draws one part's arguments, and reference() takes and returns one part's arrays. A program takes and returns all parts, laid end to end along the dimension named above; an argument that names none is the same for every part. Nothing has to cross between parts.
Inputs may be any that keep to these rules, and one draw needn't show every extreme that they name: `row_lists`: each child's list is strictly increasing and holds the first and the last root row. In each aligned run of 1024 root rows at most 256 of one child's indices fall, and exactly 256 in one run of every list.
All inputs are finite; a program needn't handle non-finite values.
Results may differ from the reference program's by a relative error of at most 0.0055.
Values may be sent and summed in bfloat16 or wider, within the bound.
No kernel may reach another device: no remote copies, remote signals or barrier semaphores. Data moves between devices by JAX's collectives and lax.ppermute only.
A program may use at most 192 MiB of HBM per device.

```python
import jax
import jax.numpy as jnp
from jax import lax

NR = 8192
NC = 8192
KC = 1024
N_ROW = 8


def pin_rank(ranks, block, spot):
    line = ranks[block]
    old = line[spot]
    line = jnp.where(line == 0, old, line)
    line = line.at[spot].set(0)
    return ranks.at[block].set(line)


def single_list(key):
    block_rows = NR // N_ROW
    most = 2 * KC // N_ROW
    second = 3 * KC // (2 * N_ROW)
    remain = KC - most - second
    base_count = remain // (N_ROW - 2)
    extra_count = remain % (N_ROW - 2)
    first_key, second_key = jax.random.split(key)
    order = jax.random.permutation(first_key, N_ROW).astype(jnp.int32)
    place = jnp.zeros((N_ROW,), jnp.int32).at[order].set(jnp.arange(N_ROW, dtype=jnp.int32))
    filler = base_count + (place - 2 < extra_count).astype(jnp.int32)
    counts = jnp.where(place == 0, most, jnp.where(place == 1, second, filler))
    block_keys = jax.random.split(second_key, N_ROW)
    ranks = jax.vmap(lambda one_key: jax.random.permutation(one_key, block_rows))(block_keys).astype(jnp.int32)
    ranks = pin_rank(ranks, 0, 0)
    ranks = pin_rank(ranks, N_ROW - 1, block_rows - 1)
    chosen = (ranks < counts[:, None]).reshape(-1)
    picked = jnp.nonzero(chosen, size=KC, fill_value=0)[0]
    return picked.astype(jnp.int32)


def draw_row_lists(key, part):
    first = single_list(jax.random.fold_in(key, 11))
    second = single_list(jax.random.fold_in(key, 23))
    return jnp.stack([first, second])


def block_scale(rng, shape, cuts, smallest, top_value):
    gain = 1.0
    for axis_at, blocks in cuts:
        heights = jax.random.uniform(jax.random.fold_in(jax.random.fold_in(rng, 6), axis_at), (blocks,), jnp.float32, smallest / len(cuts), top_value / len(cuts))
        gain = gain * jnp.repeat(jnp.exp(heights), shape[axis_at] // blocks).reshape((-1,) + (1,) * (len(shape) - 1 - axis_at))
    return gain


def normal_values(stream_key, shape, scale, reach, cuts=(), held_as=jnp.bfloat16):
    array = jax.random.normal(stream_key, shape, jnp.float32) * scale
    if len(cuts) > 0:
        array = block_scale(stream_key, shape, cuts, -0.22, 0.18) * array
    return jnp.clip(array, min=-reach, max=reach).astype(held_as)


def setup_inputs(seed: int = 0, part: int = 0) -> dict:
    streams_of = jax.random.split(jax.random.key(seed), 5)
    own_keys = jax.random.split(jax.random.fold_in(streams_of[4], part), 5)
    return {
        "root_inverse": normal_values(own_keys[0], (NR, NR), 1.0, 6.0, ((0, 8), (1, 2))),
        "panels": normal_values(own_keys[1], (2, KC, NC), KC ** -0.5, 0.1875, ((0, 2), (2, 8))),
        "diag_inverse": normal_values(own_keys[2], (2, NC, NC), 1.0, 6.0, ((0, 2), (1, 8))),
        "row_lists": draw_row_lists(jax.random.fold_in(streams_of[4], 71), part),
    }


def wide_dot(left, right):
    return jnp.dot(left.astype(jnp.float32), right.astype(jnp.float32), precision=lax.Precision.HIGHEST)


def one_child(root_inverse, panel, diag_block, rows):
    root_part = jnp.take(jnp.take(root_inverse, rows, axis=0), rows, axis=1)
    offdiag = (-wide_dot(root_part, panel)).astype(jnp.bfloat16)
    update = wide_dot(offdiag.T, panel)
    block = (diag_block.astype(jnp.float32) - update).astype(jnp.bfloat16)
    block = lax.optimization_barrier(block)
    wide = block.astype(jnp.float32)
    result = ((wide + wide.T) * 0.5).astype(jnp.bfloat16)
    return offdiag, result


def reference(root_inverse, panels, diag_inverse, row_lists):
    first_off, first_diag = one_child(root_inverse, panels[0], diag_inverse[0], row_lists[0].astype(jnp.int32))
    second_off, second_diag = one_child(root_inverse, panels[1], diag_inverse[1], row_lists[1].astype(jnp.int32))
    return jnp.stack([first_off, second_off]), jnp.stack([first_diag, second_diag])
```

```python
import functools

import jax
import jax.numpy as jnp
from jax import lax
from jax.experimental import pallas as pl
from jax.experimental.pallas import tpu as pltpu
from jax.sharding import PartitionSpec as P

VMEM_BYTES = 48 * 1024 * 1024


def pair_kernel(where, left, right, mine, theirs, *rest, send):
    result, out = (rest[-2], rest[-1]) if send else (rest[-1], None)
    total = jnp.dot(left[...], right[...], preferred_element_type=jnp.float32)
    swapped = theirs[...].astype(jnp.float32).T
    value = total + 0.5 * (mine[...].astype(jnp.float32) + swapped)
    result[...] = value.astype(jnp.bfloat16)
    if send:
        out[...] = value.T.astype(jnp.bfloat16)


def pair_block(where, left, right, diag, theirs, result, send):
    size, depth = left.shape
    tile = min(256, size)
    steps = size // tile
    shape = jax.ShapeDtypeStruct(diag.shape, jnp.bfloat16)
    in_specs = [
        pl.BlockSpec((size, depth), lambda t, w: (0, 0)),
        pl.BlockSpec((depth, tile), lambda t, w: (0, t)),
        pl.BlockSpec((size, tile), lambda t, w: (0, w[0] * steps + t)),
        pl.BlockSpec((tile, size), lambda t, w: (t, 0)),
    ]
    operands = [where, left, right, diag, theirs]
    if theirs is diag:
        in_specs[3] = pl.BlockSpec((tile, size), lambda t, w: (t, w[0]))
    aliases = {}
    if result is not None:
        in_specs.append(pl.BlockSpec(memory_space=pl.ANY))
        aliases = {len(operands): 0}
        operands.append(result)
    out_specs = [pl.BlockSpec((size, tile), lambda t, w: (0, w[0] * steps + t))]
    out_shape = [shape]
    if send:
        out_specs.append(pl.BlockSpec((tile, size), lambda t, w: (t, 0)))
        out_shape.append(jax.ShapeDtypeStruct((size, size), jnp.bfloat16))
    moved = 2 * (2 * size * depth + (4 if send else 3) * size * size)
    return pl.pallas_call(
        functools.partial(pair_kernel, send=send),
        grid_spec=pltpu.PrefetchScalarGridSpec(
            num_scalar_prefetch=1, grid=(steps,), in_specs=in_specs, out_specs=out_specs
        ),
        out_shape=out_shape,
        input_output_aliases=aliases,
        compiler_params=pltpu.CompilerParams(vmem_limit_bytes=VMEM_BYTES),
        cost_estimate=pl.CostEstimate(
            flops=2 * size * size * depth, bytes_accessed=moved, transcendentals=0
        ),
        name="pair_send" if send else "pair_keep",
    )(*operands)


def place_kernel(where, arrived, current, out):
    keep = where[1] == 1

    @pl.when(keep)
    def _():
        out[...] = current[...]

    @pl.when(jnp.logical_not(keep))
    def _():
        out[...] = arrived[...]


def place_block(where, arrived, result):
    size = arrived.shape[0]
    tile = min(256, size)
    spec = pl.BlockSpec((tile, size), lambda t, w: (t, w[0]))
    return pl.pallas_call(
        place_kernel,
        grid_spec=pltpu.PrefetchScalarGridSpec(
            num_scalar_prefetch=1,
            grid=(size // tile,),
            in_specs=[pl.BlockSpec((tile, size), lambda t, w: (t, 0)), spec],
            out_specs=spec,
        ),
        out_shape=jax.ShapeDtypeStruct(result.shape, result.dtype),
        input_output_aliases={2: 0},
        compiler_params=pltpu.CompilerParams(vmem_limit_bytes=VMEM_BYTES),
        cost_estimate=pl.CostEstimate(
            flops=0, bytes_accessed=6 * size * size, transcendentals=0
        ),
        name="place",
    )(where, arrived, result)


def pick_listed(root_block, rows, row_index, col_index, most):
    block_rows, half_cols = root_block.shape
    lower = row_index * block_rows
    first = jnp.sum((rows < lower).astype(jnp.int32))
    padded = jnp.concatenate([rows, jnp.full((most,), jnp.iinfo(jnp.int32).max, jnp.int32)])
    local_rows = lax.dynamic_slice_in_dim(padded, first, most) - lower
    take_rows = (
        local_rows[:, None] == lax.broadcasted_iota(jnp.int32, (most, block_rows), 1)
    ).astype(jnp.bfloat16)
    taken = jnp.dot(take_rows, root_block, preferred_element_type=jnp.float32)
    local_cols = rows - col_index * half_cols
    take_cols = (
        local_cols[None, :] == lax.broadcasted_iota(jnp.int32, (half_cols, rows.shape[0]), 0)
    ).astype(jnp.bfloat16)
    picked = jnp.dot(
        taken.astype(jnp.bfloat16), take_cols, preferred_element_type=jnp.float32
    )
    return picked.astype(jnp.bfloat16)


def per_device(root_inverse, panels, diag_inverse, row_lists):
    row_index = lax.axis_index("row")
    col_index = lax.axis_index("col")
    n_rows = lax.axis_size("row")
    n_cols = lax.axis_size("col")
    half = n_rows // 2
    listed = row_lists.shape[1]
    most = 2 * listed // n_rows
    block_rows = root_inverse.shape[0]
    panel = panels[0]
    diag = diag_inverse[0]
    size = diag.shape[0]
    computes = (row_index // half == col_index).astype(jnp.int32)

    def side(row, col):
        return row // half == col

    def swap(value, step, sender):
        pairs = [
            (row * n_cols + col, (row ^ step) * n_cols + col)
            for row in range(n_rows)
            for col in range(n_cols)
            if sender is None or side(row, col) == sender
        ]
        return lax.ppermute(value, ("row", "col"), pairs)

    def wanted(step):
        return lax.dynamic_slice_in_dim(diag, (row_index ^ step) * size, size, 1)

    held = {0: panel}
    held[half] = swap(panel, half, False)
    step = half // 2
    while step >= 1:
        for slot in sorted(held, reverse=True):
            held[slot ^ step] = swap(held[slot], step, True if slot >= half else None)
        step //= 2

    theirs = {0: diag}
    for step in range(n_rows - 1, 0, -1):
        theirs[step] = swap(wanted(step), step, False if step >= half else None)

    other_rows = lax.dynamic_index_in_dim(row_lists, 1 - col_index, 0, keepdims=False)
    child_rows = lax.dynamic_index_in_dim(row_lists, col_index, 0, keepdims=False)
    for_other = pick_listed(root_inverse, other_rows, row_index, col_index, most)
    from_other = lax.ppermute(for_other, "col", [(0, 1), (1, 0)])
    own = pick_listed(root_inverse, child_rows, row_index, col_index, most) + from_other
    pieces = {0: own}
    step = half
    while step >= 1:
        for slot in list(pieces):
            pieces[slot ^ step] = swap(pieces[slot], step, None)
        step //= 2
    stacked = jnp.concatenate([pieces[slot] for slot in range(n_rows)], axis=0)
    owners = child_rows // block_rows
    bounds = jnp.arange(n_rows, dtype=jnp.int32) * block_rows
    starts = jnp.sum((child_rows[None, :] < bounds[:, None]).astype(jnp.int32), axis=1)
    begun = jnp.sum(
        jnp.where(owners[:, None] == jnp.arange(n_rows, dtype=jnp.int32)[None, :], starts[None, :], 0),
        axis=1,
    )
    ranking = jnp.arange(listed, dtype=jnp.int32) - begun
    place = (owners ^ row_index) * most + ranking
    chosen = (
        place[:, None] == lax.broadcasted_iota(jnp.int32, (listed, n_rows * most), 1)
    ).astype(jnp.bfloat16)
    root_part = jnp.dot(chosen, stacked, preferred_element_type=jnp.float32).astype(jnp.bfloat16)

    offdiag = (-jnp.dot(root_part, panel, preferred_element_type=jnp.float32)).astype(jnp.bfloat16)
    straight = lax.dot_general(
        panel, root_part, (((0,), (1,)), ((), ())), preferred_element_type=jnp.float32
    )
    crossed = lax.dot_general(
        panel, root_part, (((0,), (0,)), ((), ())), preferred_element_type=jnp.float32
    )
    left = (0.5 * (straight + crossed)).astype(jnp.bfloat16)

    result = None
    returned = {}
    order = list(range(half)) + list(range(half, n_rows))
    for step in order:
        where = jnp.stack([row_index ^ step, computes])
        outs = pair_block(where, left, held[step], diag, theirs[step], result, step >= half)
        result = outs[0]
        if step >= half:
            returned[step] = swap(outs[1], step, True)
    for step in range(half, n_rows):
        where = jnp.stack([row_index ^ step, computes])
        result = place_block(where, returned[step], result)
    return (offdiag[None], result[None])


def solution(mesh):
    placed = (
        P(("poles", "row"), "col"),
        P(("poles", "col"), None, "row"),
        P(("poles", "col"), "row", None),
        P(),
    )

    return jax.shard_map(
        per_device,
        mesh=mesh,
        in_specs=placed,
        out_specs=(P(("poles", "col"), None, "row"), P(("poles", "col"), "row", None)),
        check_vma=False,
    )
```
